32 devices in a mesh: shot: 4 (over x, core), tile: 8 (over z, y).
Axes of the slice: x: 2, y: 2, z: 4, core: 2. Of those that a mesh axis runs over, the one named last changes fastest.
Arguments:
- adjoint_now: float32 [4, 64, 64, 128], P('shot', 'tile'), may hold values from -6 to 6
- adjoint_prev: float32 [4, 64, 64, 128], P('shot', 'tile'), may hold values from -6 to 6
- costates: float32 [4, 6, 64, 64, 128], P('shot', None, 'tile'), may hold values from -6 to 6
- modulus: float32 [64, 64, 128], P('tile'), may hold values from 0.04 to 0.2
- relaxation: float32 [64, 64, 128], P('tile'), may hold values from 0.1 to 0.6
- absorb_mask: int32 [64, 64, 128], P('tile'), may hold values from 0 to 1, as said below
- relax_rates: float32 [6], replicated, may hold values from 0.02 to 2
- mech_weights: float32 [6], replicated, may hold values from 0.1 to 1
- forward_lap: bfloat16 [4, 6, 64, 64, 128], P('shot', None, 'tile'), may hold values from -0.59765625 to 0.59765625
- recv_cells: int32 [4, 512], P('shot'), may hold values from 0 to 524287
- enc_signs: int32 [4, 8], P('shot'), may hold values from -1 to 1, as said below
- residuals: float32 [4, 8, 6, 512], P('shot'), may hold values from -6 to 6
Outputs:
- adjoint_out: float32 [4, 64, 64, 128], P('shot', 'tile')
- grad_modulus: float32 [64, 64, 128], P('tile', 'shot')
- grad_relax: float32 [64, 64, 128], P('tile', 'shot')
The draws below stay inside these ranges and needn't reach their ends.
Inputs may be any that keep to these rules, and one draw needn't show every extreme that they name: absorb_mask is 1 in layers along all six faces of the grid, each 1 to 8 cells thick and at most a quarter of the grid's extent, and 0 inside. `enc_signs`: each entry is -1 or +1.
All inputs are finite; a program needn't handle non-finite values.
Results may differ from the reference program's by a relative error of at most 0.00055.
Values sent between devices are 32-bit elements; how exact they have to be, the bound alone decides.
A program may use at most 64 MiB of HBM per device.

```python
import math
import jax
import jax.numpy as jnp
from jax import lax

CY = 64
CZ = 128
STEPS = 6
MECHS = 6
ENCODED = 8
RECEIVERS = 512
GROUPS = 4
NX = 64


def draw_absorb_mask(key, part):
    keys = jax.random.split(key, 3)
    width_x = jax.random.randint(keys[0], (), 1, min(8, NX // 4) + 1)
    width_y = jax.random.randint(keys[1], (), 1, min(8, CY // 4) + 1)
    width_z = jax.random.randint(keys[2], (), 1, min(8, CZ // 4) + 1)
    index_x = jnp.arange(NX)[:, None, None]
    index_y = jnp.arange(CY)[None, :, None]
    index_z = jnp.arange(CZ)[None, None, :]
    layer_x = (index_x < width_x) | (index_x >= NX - width_x)
    layer_y = (index_y < width_y) | (index_y >= CY - width_y)
    layer_z = (index_z < width_z) | (index_z >= CZ - width_z)
    return (layer_x | layer_y | layer_z).astype(jnp.int32)


def draw_enc_signs(key, part):
    return 2 * jax.random.randint(key, (GROUPS, ENCODED), 0, 2) - 1


def place_ends(array, own_key, least, largest):
    index_at = [jax.random.randint(jax.random.fold_in(own_key, axis), (), 0, length) for axis, length in enumerate(array.shape)]
    longest = array.shape.index(max(array.shape))
    beside = index_at[:longest] + [(index_at[longest] + 1) % array.shape[longest]] + index_at[longest + 1:]
    return array.at[tuple(index_at)].set(least).at[tuple(beside)].set(largest)


def level_of(rng, extent, cuts, smallest, high):
    factor_of = 1.0
    for dim, shards_of in cuts:
        heights = jax.random.uniform(jax.random.fold_in(jax.random.fold_in(rng, 6), dim), (shards_of,), jnp.float32, smallest / len(cuts), high / len(cuts))
        factor_of = factor_of * jnp.repeat(jnp.exp(heights), extent[dim] // shards_of).reshape((-1,) + (1,) * (len(extent) - 1 - dim))
    return factor_of


def centred(own_key, shape, deviation, most, cuts=(), dtype=jnp.bfloat16):
    factor_of = level_of(own_key, shape, cuts, -0.22, 0.18) if cuts else 1.0
    values = jax.random.normal(own_key, shape, jnp.float32) * deviation * factor_of
    return jnp.minimum(jnp.maximum(values, -most), most).astype(dtype)


def setup_inputs(seed: int = 0) -> dict:
    key_of = jax.random.split(jax.random.key(seed), 13)
    return {
        "adjoint_now": centred(key_of[0], (GROUPS, NX, CY, CZ), 1.0, 6.0, ((0, 4), (1, 8)), jnp.float32),
        "adjoint_prev": centred(key_of[1], (GROUPS, NX, CY, CZ), 1.0, 6.0, ((0, 4), (1, 8)), jnp.float32),
        "costates": centred(key_of[2], (GROUPS, MECHS, NX, CY, CZ), 1.0, 6.0, ((0, 4), (2, 8)), jnp.float32),
        "modulus": jnp.clip(0.04 + 0.16 * jax.random.uniform(key_of[3], (NX, CY, CZ), jnp.float32) ** level_of(key_of[3], (NX, CY, CZ), ((0, 8),), -0.2, 0.2), 0.04, 0.2),
        "relaxation": jnp.clip(0.1 + 0.5 * jax.random.uniform(key_of[4], (NX, CY, CZ), jnp.float32) ** level_of(key_of[4], (NX, CY, CZ), ((0, 8),), -0.2, 0.2), 0.1, 0.6),
        "absorb_mask": draw_absorb_mask(jax.random.fold_in(key_of[12], 71), 0),
        "relax_rates": jnp.clip(jnp.exp(jax.random.uniform(key_of[6], (MECHS,), jnp.float32, math.log(0.02), math.log(2.0))), 0.02, 2.0),
        "mech_weights": jnp.clip(jnp.exp(jax.random.uniform(key_of[7], (MECHS,), jnp.float32, math.log(0.1), math.log(1.0))), 0.1, 1.0),
        "forward_lap": centred(key_of[8], (GROUPS, STEPS, NX, CY, CZ), 0.1, 0.59765625, ((0, 4), (2, 8))),
        "recv_cells": place_ends(jax.random.randint(key_of[9], (GROUPS, RECEIVERS), 0, NX * CY * CZ), jax.random.fold_in(key_of[9], 1), 0, (NX * CY * CZ) - 1).astype(jnp.int32),
        "enc_signs": draw_enc_signs(jax.random.fold_in(key_of[12], 71), 0),
        "residuals": centred(key_of[11], (GROUPS, ENCODED, STEPS, RECEIVERS), 1.0, 6.0, ((0, 4),), jnp.float32),
    }


coeffs = (-205.0 / 72.0, 8.0 / 5.0, -1.0 / 5.0, 8.0 / 315.0, -1.0 / 560.0)
damping = 0.2


def laplace_eight(field):
    size_x, size_y, size_z = field.shape
    padded = jnp.pad(field, 4)
    center = padded[4:4 + size_x, 4:4 + size_y, 4:4 + size_z]
    result = 3.0 * coeffs[0] * center
    for offset in range(1, 5):
        result = result + coeffs[offset] * (padded[4 + offset:4 + offset + size_x, 4:4 + size_y, 4:4 + size_z] + padded[4 - offset:4 - offset + size_x, 4:4 + size_y, 4:4 + size_z])
        result = result + coeffs[offset] * (padded[4:4 + size_x, 4 + offset:4 + offset + size_y, 4:4 + size_z] + padded[4:4 + size_x, 4 - offset:4 - offset + size_y, 4:4 + size_z])
        result = result + coeffs[offset] * (padded[4:4 + size_x, 4:4 + size_y, 4 + offset:4 + offset + size_z] + padded[4:4 + size_x, 4:4 + size_y, 4 - offset:4 - offset + size_z])
    return result


def reference(adjoint_now, adjoint_prev, costates, modulus, relaxation, absorb_mask, relax_rates, mech_weights, forward_lap, recv_cells, enc_signs, residuals):
    decay = jnp.exp(-relax_rates)[:, None, None, None]
    weights = mech_weights[:, None, None, None]
    damp = 1.0 - damping * absorb_mask.astype(jnp.float32)

    def one_group(carry, items):
        grad_m, grad_t = carry
        current, previous, memory, snaps, cells, signs, resid = items
        sources = jnp.sum(signs.astype(jnp.float32)[:, None, None] * resid, axis=0)
        for step_index in range(STEPS - 1, -1, -1):
            summed = jnp.sum(weights * memory, axis=0)
            stress = modulus * (current - relaxation * summed)
            lap = laplace_eight(stress)
            memory = decay * memory + (1.0 - decay) * current[None]
            inject = jnp.zeros((NX * CY * CZ,), jnp.float32).at[cells].add(sources[step_index]).reshape(NX, CY, CZ)
            fresh = damp * (2.0 * current - previous + lap + inject)
            previous = current
            current = fresh
            snap = snaps[step_index].astype(jnp.float32)
            grad_m = grad_m + current * snap
            grad_t = grad_t + modulus * jnp.sum(weights * memory, axis=0) * snap
        return (grad_m, grad_t), current

    start = (jnp.zeros((NX, CY, CZ), jnp.float32), jnp.zeros((NX, CY, CZ), jnp.float32))
    (grad_m, grad_t), finals = lax.scan(one_group, start, (adjoint_now, adjoint_prev, costates, forward_lap, recv_cells, enc_signs, residuals))
    return finals, grad_m, grad_t
```

```python
import functools

import jax
import jax.numpy as jnp
from jax import lax
from jax.experimental import pallas as pl
from jax.experimental.pallas import tpu as pltpu
from jax.sharding import PartitionSpec as P

MESH = pl.DeviceIdType.MESH
coeffs = (-205.0 / 72.0, 8.0 / 5.0, -1.0 / 5.0, 8.0 / 315.0, -1.0 / 560.0)
damping = 0.2
CHUNKS = 4
PAD = 8


def kernel(
    shots,
    tiles,
    now_ref,
    prev_ref,
    cost_ref,
    mod_ref,
    relax_ref,
    mask_ref,
    rates_ref,
    weights_ref,
    snaps_ref,
    cells_ref,
    signs_ref,
    resid_ref,
    out_ref,
    own_m_ref,
    own_t_ref,
    stress,
    halo,
    memory,
    adj,
    prev,
    damp,
    base,
    relaxed,
    grad_m,
    grad_t,
    send_m,
    send_t,
    got_m,
    got_t,
    parts,
    low_hot,
    vecs,
    halo_send,
    halo_recv,
    m_send,
    m_recv,
    t_send,
    t_recv,
):
    steps = snaps_ref.shape[1]
    mechs = cost_ref.shape[1]
    rows, cols, depth = mod_ref.shape
    half = rows // 2
    wide = cols // CHUNKS
    per = shots // CHUNKS
    owned = cols // shots
    receivers = cells_ref.shape[1]
    me = lax.axis_index("shot")
    tile = lax.axis_index("tile")
    has = (tile > 0, tile < tiles - 1)
    partner = (tile - 1, tile + 1)

    barrier = pltpu.get_barrier_semaphore()
    for side in range(2):

        @pl.when(has[side])
        def _(side=side):
            pl.semaphore_signal(barrier, inc=1, device_id={"tile": partner[side]}, device_id_type=MESH)

    for away in range(1, shots):
        pl.semaphore_signal(
            barrier, inc=1, device_id={"shot": lax.rem(me + away, shots)}, device_id_type=MESH
        )

    def halo_copy(k, side, start):
        return pltpu.make_async_remote_copy(
            src_ref=stress.at[k, pl.ds(side * half, half), pl.ds(pl.multiple_of(start + PAD, 8), wide), :],
            dst_ref=halo.at[k, 1 - side, :, pl.ds(start, wide), :],
            send_sem=halo_send.at[k, side, start // wide],
            recv_sem=halo_recv.at[k, 1 - side, start // wide],
            device_id={"tile": partner[side]},
            device_id_type=MESH,
        )

    def send_halo(k, side, start):
        @pl.when(has[side])
        def _():
            halo_copy(k, side, start).start()

    def wait_halo(k, side, start):
        @pl.when(has[side])
        def _():
            pltpu.make_async_remote_copy(
                src_ref=stress.at[k, pl.ds(side * half, half), pl.ds(pl.multiple_of(start + PAD, 8), wide), :],
                dst_ref=halo.at[k, side, :, pl.ds(start, wide), :],
                send_sem=halo_send.at[k, side, start // wide],
                recv_sem=halo_recv.at[k, side, start // wide],
                device_id={"tile": partner[side]},
                device_id_type=MESH,
            ).wait_recv()

    def m_copy(owner, source, side):
        return pltpu.make_async_remote_copy(
            src_ref=send_m.at[owner, pl.ds(side * half, half)],
            dst_ref=got_m.at[source, pl.ds(side * half, half)],
            send_sem=m_send.at[owner, side],
            recv_sem=m_recv.at[source, side],
            device_id={"shot": owner},
            device_id_type=MESH,
        )

    def t_copy(owner, source):
        return pltpu.make_async_remote_copy(
            src_ref=send_t.at[owner],
            dst_ref=got_t.at[source],
            send_sem=t_send.at[owner],
            recv_sem=t_recv.at[source],
            device_id={"shot": owner},
            device_id_type=MESH,
        )

    first = lax.rem(me // per + 1, CHUNKS)

    def chunk_of(c):
        return lax.rem(first + c, CHUNKS)

    for m in range(mechs):
        decay = jnp.exp(jnp.full((1, depth), -rates_ref[m], jnp.float32))
        weight = jnp.full((1, depth), weights_ref[m], jnp.float32)
        vecs[m] = decay
        vecs[mechs + m] = weight * (1.0 - decay)
        vecs[2 * mechs + m] = weight
    lane = lax.broadcasted_iota(jnp.int32, (1, depth), 1)
    for k in range(1, 5):
        vecs[3 * mechs + k - 1] = jnp.where(lane >= k, coeffs[k], 0.0)
        vecs[3 * mechs + 3 + k] = jnp.where(lane < depth - k, coeffs[k], 0.0)

    def begin(c, carry):
        chunk = chunk_of(c)
        start = pl.multiple_of(chunk * wide, wide)
        at = pl.ds(start, wide)
        padded = pl.ds(pl.multiple_of(start + PAD, 8), wide)
        total = None
        for m in range(mechs):
            value = vecs[2 * mechs + m] * cost_ref[0, m, :, at, :]
            memory[m, :, at, :] = value
            total = value if total is None else total + value
        now = now_ref[0, :, at, :]
        adj[:, at, :] = now
        stress[0, :, padded, :] = mod_ref[:, at, :] * (now - relax_ref[:, at, :] * total)
        return carry

    lax.fori_loop(0, CHUNKS, begin, 0)

    peers = shots - 1 + has[0].astype(jnp.int32) + has[1].astype(jnp.int32)
    pl.semaphore_wait(barrier, peers)

    def begin_send(c, carry):
        start = pl.multiple_of(chunk_of(c) * wide, wide)
        for side in range(2):
            send_halo(0, side, start)
        return carry

    lax.fori_loop(0, CHUNKS, begin_send, 0)

    empty = jnp.zeros((rows, PAD, depth), jnp.float32)

    def clear(k, carry):
        stress[k, :, 0:PAD, :] = empty
        stress[k, :, PAD + cols :, :] = empty
        for side in range(2):

            @pl.when(jnp.logical_not(has[side]))
            def _(side=side):
                halo[k, side] = jnp.zeros((half, cols, depth), jnp.float32)

        return carry

    lax.fori_loop(0, steps, clear, 0)

    sources = None
    for e in range(signs_ref.shape[1]):
        term = signs_ref[0, e].astype(jnp.float32) * resid_ref[0, e]
        sources = term if sources is None else sources + term
    for p in range(3):
        piece = sources.astype(jnp.bfloat16).astype(jnp.float32)
        for k in range(steps):
            parts[k, p : p + 1, :] = piece[steps - 1 - k : steps - k]
        sources = sources - piece
    cell = cells_ref[...] - tile * (rows * cols * depth)
    high = cell >> 7
    low = cell & 127
    low_hot[...] = jnp.where(
        lax.broadcasted_iota(jnp.int32, (depth, receivers), 0) == low, 1.0, 0.0
    ).astype(jnp.bfloat16)

    def prepare(c, carry):
        at = pl.ds(pl.multiple_of(c * wide, wide), wide)
        damp[:, at, :] = 1.0 - damping * mask_ref[:, at, :].astype(jnp.float32)
        prev[:, at, :] = prev_ref[0, :, at, :]
        grad_m[:, at, :] = jnp.zeros((rows, wide, depth), jnp.float32)
        grad_t[:, at, :] = jnp.zeros((rows, wide, depth), jnp.float32)
        return carry

    lax.fori_loop(0, CHUNKS, prepare, 0)

    def before(k, c, last):
        chunk = chunk_of(c)
        start = pl.multiple_of(chunk * wide, wide)
        at = pl.ds(start, wide)
        index = lax.broadcasted_iota(jnp.int32, (rows * wide, receivers), 0)
        spot = (index // wide) * cols + lax.rem(index, wide) + start
        hot = spot == high
        inject = None
        for p in range(3):
            left = jnp.where(hot, parts[k, p : p + 1, :], 0.0).astype(jnp.bfloat16)
            term = lax.dot_general(
                left, low_hot[...], (((1,), (1,)), ((), ())), preferred_element_type=jnp.float32
            )
            inject = term if inject is None else inject + term
        inject = inject.reshape(rows, wide, depth)
        window = stress[k, :, pl.ds(start, wide + 2 * PAD), :]
        center = window[:, PAD : PAD + wide]
        zeros = jnp.zeros((4, wide, depth), jnp.float32)
        tall = jnp.concatenate([zeros, center, zeros], axis=0)
        lap = (3.0 * coeffs[0]) * center
        for j in range(1, 5):
            near = window[:, PAD + j : PAD + j + wide] + window[:, PAD - j : PAD - j + wide]
            near = near + (tall[4 + j : 4 + j + rows] + tall[4 - j : 4 - j + rows])
            lap = lap + coeffs[j] * near
            lap = lap + vecs[3 * mechs + j - 1] * pltpu.roll(center, j, 2)
            lap = lap + vecs[3 * mechs + 3 + j] * pltpu.roll(center, depth - j, 2)
        now = adj[:, at, :]
        base[:, at, :] = damp[:, at, :] * (2.0 * now - prev[:, at, :] + lap + inject)
        prev[:, at, :] = now
        total = None
        for m in range(mechs):
            value = vecs[m] * memory[m, :, at, :] + vecs[mechs + m] * now
            memory[m, :, at, :] = value
            total = value if total is None else total + value
        weighted = mod_ref[:, at, :] * total
        relaxed[:, at, :] = relax_ref[:, at, :] * weighted
        gained = grad_t[:, at, :] + weighted * snaps_ref[0, steps - 1 - k, :, at, :].astype(jnp.float32)
        if last:
            for i in range(per):
                owner = chunk * per + i
                send_t[owner] = gained[:, i * owned : (i + 1) * owned, :]

                @pl.when(owner != me)
                def _(owner=owner):
                    t_copy(owner, me).start()
        else:
            grad_t[:, at, :] = gained

    def after(k, c, last):
        chunk = chunk_of(c)
        start = pl.multiple_of(chunk * wide, wide)
        at = pl.ds(start, wide)
        for side in range(2):
            wait_halo(k, side, start)
            lines = pl.ds(side * half, half)
            near = halo[k, side, :, at, :]
            zeros = jnp.zeros((4, wide, depth), jnp.float32)
            extra = None
            for j in range(1, 5):
                if side == 0:
                    shifted = jnp.concatenate([near, zeros], axis=0)[4 - j : 8 - j]
                else:
                    shifted = jnp.concatenate([zeros, near], axis=0)[j : 4 + j]
                term = coeffs[j] * shifted
                extra = term if extra is None else extra + term
            fresh = base[lines, at, :] + damp[lines, at, :] * extra
            gained = grad_m[lines, at, :] + fresh * snaps_ref[0, steps - 1 - k, lines, at, :].astype(jnp.float32)
            if last:
                out_ref[0, lines, at, :] = fresh
                for i in range(per):
                    owner = chunk * per + i
                    send_m[owner, lines] = gained[:, i * owned : (i + 1) * owned, :]

                    @pl.when(owner != me)
                    def _(owner=owner, side=side):
                        m_copy(owner, me, side).start()
            else:
                padded = pl.ds(pl.multiple_of(start + PAD, 8), wide)
                stress[k + 1, lines, padded, :] = mod_ref[lines, at, :] * fresh - relaxed[lines, at, :]
                send_halo(k + 1, side, start)
                adj[lines, at, :] = fresh
                grad_m[lines, at, :] = gained

    def loop(k, body, last):
        def one(c, carry):
            body(k, c, last)
            return carry

        lax.fori_loop(0, CHUNKS, one, 0)

    def step(k, carry):
        loop(k, before, False)
        loop(k, after, False)
        return carry

    lax.fori_loop(0, steps - 1, step, 0)
    loop(steps - 1, before, True)
    loop(steps - 1, after, True)

    total_t = send_t[me]
    for away in range(1, shots):
        source = lax.rem(me + away, shots)
        t_copy(source, source).wait_recv()
        total_t = total_t + got_t[source]
    own_t_ref[...] = total_t
    total_m = send_m[me]
    for away in range(1, shots):
        source = lax.rem(me + away, shots)
        for side in range(2):
            m_copy(source, source, side).wait_recv()
        total_m = total_m + got_m[source]
    own_m_ref[...] = total_m

    def finish(k, carry):
        for side in range(2):
            for c in range(CHUNKS):

                @pl.when(has[side])
                def _():
                    halo_copy(k, side, c * wide).wait_send()

        return carry

    lax.fori_loop(0, steps, finish, 0)
    for away in range(1, shots):
        owner = lax.rem(me + away, shots)
        t_copy(owner, me).wait_send()
        for side in range(2):
            m_copy(owner, me, side).wait_send()


def solution(mesh):
    shots = mesh.shape["shot"]
    tiles = mesh.shape["tile"]

    def shards(*args):
        now, _, costates, modulus, _, _, _, _, snaps, cells, _, _ = args
        rows, cols, depth = modulus.shape
        mechs = costates.shape[1]
        steps = snaps.shape[1]
        receivers = cells.shape[1]
        owned = cols // shots
        field = pltpu.VMEM((rows, cols, depth), jnp.float32)
        blocks = pltpu.VMEM((shots, rows, owned, depth), jnp.float32)
        vmem = pl.BlockSpec(memory_space=pltpu.VMEM)
        smem = pl.BlockSpec(memory_space=pltpu.SMEM)
        return pl.pallas_call(
            functools.partial(kernel, shots, tiles),
            out_shape=(
                jax.ShapeDtypeStruct(now.shape, jnp.float32),
                jax.ShapeDtypeStruct((rows, owned, depth), jnp.float32),
                jax.ShapeDtypeStruct((rows, owned, depth), jnp.float32),
            ),
            in_specs=[vmem] * 6 + [smem] * 2 + [vmem] * 2 + [smem, vmem],
            out_specs=(vmem, vmem, vmem),
            scratch_shapes=[
                pltpu.VMEM((steps, rows, cols + 2 * PAD, depth), jnp.float32),
                pltpu.VMEM((steps, 2, rows // 2, cols, depth), jnp.float32),
                pltpu.VMEM((mechs, rows, cols, depth), jnp.float32),
                field,
                field,
                field,
                field,
                field,
                field,
                field,
                blocks,
                blocks,
                blocks,
                blocks,
                pltpu.VMEM((steps, 8, receivers), jnp.float32),
                pltpu.VMEM((depth, receivers), jnp.bfloat16),
                pltpu.VMEM((3 * mechs + 8, 1, depth), jnp.float32),
                pltpu.SemaphoreType.DMA((steps, 2, CHUNKS)),
                pltpu.SemaphoreType.DMA((steps, 2, CHUNKS)),
                pltpu.SemaphoreType.DMA((shots, 2)),
                pltpu.SemaphoreType.DMA((shots, 2)),
                pltpu.SemaphoreType.DMA((shots,)),
                pltpu.SemaphoreType.DMA((shots,)),
            ],
            compiler_params=pltpu.CompilerParams(
                collective_id=0, has_side_effects=True, vmem_limit_bytes=40 * 1024 * 1024
            ),
        )(*args)

    return jax.shard_map(
        shards,
        mesh=mesh,
        in_specs=(
            P("shot", "tile", None, None),
            P("shot", "tile", None, None),
            P("shot", None, "tile", None, None),
            P("tile", None, None),
            P("tile", None, None),
            P("tile", None, None),
            P(),
            P(),
            P("shot", None, "tile", None, None),
            P("shot", None),
            P("shot", None),
            P("shot", None, None, None),
        ),
        out_specs=(P("shot", "tile", None, None), P("tile", "shot", None), P("tile", "shot", None)),
        check_vma=False,
    )
```

```python
import functools

import jax
import jax.numpy as jnp
from jax import lax
from jax.experimental import pallas as pl
from jax.experimental.pallas import tpu as pltpu
from jax.sharding import PartitionSpec as P

MESH = pl.DeviceIdType.MESH
coeffs = (-205.0 / 72.0, 8.0 / 5.0, -1.0 / 5.0, 8.0 / 315.0, -1.0 / 560.0)
damping = 0.2
CHUNKS = 4
PAD = 8


def kernel(
    shots,
    tiles,
    now_hbm,
    prev_hbm,
    cost_hbm,
    mod_hbm,
    relax_hbm,
    mask_hbm,
    rates_ref,
    weights_ref,
    snaps_hbm,
    cells_hbm,
    signs_ref,
    resid_hbm,
    out_ref,
    own_m_ref,
    own_t_ref,
    stress,
    halo,
    memory,
    adj,
    prev,
    damp,
    base,
    relaxed,
    grad_m,
    grad_t,
    send_m,
    send_t,
    got_m,
    got_t,
    parts,
    low_hot,
    vecs,
    mod_ref,
    relax_ref,
    mask_ref,
    snaps_ref,
    cells_ref,
    resid_ref,
    loads,
    halo_send,
    halo_recv,
    m_send,
    m_recv,
    t_send,
    t_recv,
):
    steps = snaps_ref.shape[0]
    mechs = memory.shape[0]
    rows, cols, depth = mod_ref.shape
    half = rows // 2
    wide = cols // CHUNKS
    per = shots // CHUNKS
    owned = cols // shots
    receivers = cells_ref.shape[1]
    me = lax.axis_index("shot")
    tile = lax.axis_index("tile")
    has = (tile > 0, tile < tiles - 1)
    partner = (tile - 1, tile + 1)

    staged = [
        pltpu.make_async_copy(source, target, loads.at[i])
        for i, (source, target) in enumerate(
            (
                (cost_hbm.at[0], memory),
                (now_hbm.at[0], adj),
                (mod_hbm, mod_ref),
                (relax_hbm, relax_ref),
                (cells_hbm, cells_ref),
                (resid_hbm.at[0], resid_ref),
                (mask_hbm, mask_ref),
                (prev_hbm.at[0], prev),
                (snaps_hbm.at[0], snaps_ref),
            )
        )
    ]
    for load in staged:
        load.start()

    barrier = pltpu.get_barrier_semaphore()
    for side in range(2):

        @pl.when(has[side])
        def _(side=side):
            pl.semaphore_signal(barrier, inc=1, device_id={"tile": partner[side]}, device_id_type=MESH)

    for away in range(1, shots):
        pl.semaphore_signal(
            barrier, inc=1, device_id={"shot": lax.rem(me + away, shots)}, device_id_type=MESH
        )

    def halo_copy(k, side, start):
        return pltpu.make_async_remote_copy(
            src_ref=stress.at[k, pl.ds(side * half, half), pl.ds(pl.multiple_of(start + PAD, 8), wide), :],
            dst_ref=halo.at[k, 1 - side, :, pl.ds(start, wide), :],
            send_sem=halo_send.at[k, side, start // wide],
            recv_sem=halo_recv.at[k, 1 - side, start // wide],
            device_id={"tile": partner[side]},
            device_id_type=MESH,
        )

    def send_halo(k, side, start):
        @pl.when(has[side])
        def _():
            halo_copy(k, side, start).start()

    def wait_halo(k, side, start):
        @pl.when(has[side])
        def _():
            pltpu.make_async_remote_copy(
                src_ref=stress.at[k, pl.ds(side * half, half), pl.ds(pl.multiple_of(start + PAD, 8), wide), :],
                dst_ref=halo.at[k, side, :, pl.ds(start, wide), :],
                send_sem=halo_send.at[k, side, start // wide],
                recv_sem=halo_recv.at[k, side, start // wide],
                device_id={"tile": partner[side]},
                device_id_type=MESH,
            ).wait_recv()

    def m_copy(owner, source, side):
        return pltpu.make_async_remote_copy(
            src_ref=send_m.at[owner, pl.ds(side * half, half)],
            dst_ref=got_m.at[source, pl.ds(side * half, half)],
            send_sem=m_send.at[owner, side],
            recv_sem=m_recv.at[source, side],
            device_id={"shot": owner},
            device_id_type=MESH,
        )

    def t_copy(owner, source):
        return pltpu.make_async_remote_copy(
            src_ref=send_t.at[owner],
            dst_ref=got_t.at[source],
            send_sem=t_send.at[owner],
            recv_sem=t_recv.at[source],
            device_id={"shot": owner},
            device_id_type=MESH,
        )

    first = lax.rem(me // per + 1, CHUNKS)

    def chunk_of(c):
        return lax.rem(first + c, CHUNKS)

    for m in range(mechs):
        decay = jnp.exp(jnp.full((1, depth), -rates_ref[m], jnp.float32))
        weight = jnp.full((1, depth), weights_ref[m], jnp.float32)
        vecs[m] = decay
        vecs[mechs + m] = weight * (1.0 - decay)
        vecs[2 * mechs + m] = weight
    lane = lax.broadcasted_iota(jnp.int32, (1, depth), 1)
    for k in range(1, 5):
        vecs[3 * mechs + k - 1] = jnp.where(lane >= k, coeffs[k], 0.0)
        vecs[3 * mechs + 3 + k] = jnp.where(lane < depth - k, coeffs[k], 0.0)

    for load in staged[:4]:
        load.wait()

    def begin(c, carry):
        chunk = chunk_of(c)
        start = pl.multiple_of(chunk * wide, wide)
        at = pl.ds(start, wide)
        padded = pl.ds(pl.multiple_of(start + PAD, 8), wide)
        total = None
        for m in range(mechs):
            value = vecs[2 * mechs + m] * memory[m, :, at, :]
            memory[m, :, at, :] = value
            total = value if total is None else total + value
        now = adj[:, at, :]
        stress[0, :, padded, :] = mod_ref[:, at, :] * (now - relax_ref[:, at, :] * total)
        return carry

    lax.fori_loop(0, CHUNKS, begin, 0)

    peers = shots - 1 + has[0].astype(jnp.int32) + has[1].astype(jnp.int32)
    pl.semaphore_wait(barrier, peers)

    def begin_send(c, carry):
        start = pl.multiple_of(chunk_of(c) * wide, wide)
        for side in range(2):
            send_halo(0, side, start)
        return carry

    lax.fori_loop(0, CHUNKS, begin_send, 0)

    empty = jnp.zeros((rows, PAD, depth), jnp.float32)

    def clear(k, carry):
        stress[k, :, 0:PAD, :] = empty
        stress[k, :, PAD + cols :, :] = empty
        for side in range(2):

            @pl.when(jnp.logical_not(has[side]))
            def _(side=side):
                halo[k, side] = jnp.zeros((half, cols, depth), jnp.float32)

        return carry

    lax.fori_loop(0, steps, clear, 0)

    for load in staged[4:6]:
        load.wait()
    sources = None
    for e in range(signs_ref.shape[1]):
        term = signs_ref[0, e].astype(jnp.float32) * resid_ref[:, e]
        sources = term if sources is None else sources + term
    for p in range(3):
        piece = sources.astype(jnp.bfloat16).astype(jnp.float32)
        for k in range(steps):
            parts[k, p : p + 1, :] = piece[steps - 1 - k : steps - k]
        sources = sources - piece
    cell = cells_ref[...] - tile * (rows * cols * depth)
    high = cell >> 7
    low = cell & 127
    low_hot[...] = jnp.where(
        lax.broadcasted_iota(jnp.int32, (depth, receivers), 0) == low, 1.0, 0.0
    ).astype(jnp.bfloat16)

    for load in staged[6:]:
        load.wait()

    def prepare(c, carry):
        at = pl.ds(pl.multiple_of(c * wide, wide), wide)
        damp[:, at, :] = 1.0 - damping * mask_ref[:, at, :].astype(jnp.float32)
        grad_m[:, at, :] = jnp.zeros((rows, wide, depth), jnp.float32)
        grad_t[:, at, :] = jnp.zeros((rows, wide, depth), jnp.float32)
        return carry

    lax.fori_loop(0, CHUNKS, prepare, 0)

    def before(k, c, last):
        chunk = chunk_of(c)
        start = pl.multiple_of(chunk * wide, wide)
        at = pl.ds(start, wide)
        index = lax.broadcasted_iota(jnp.int32, (rows * wide, receivers), 0)
        spot = (index // wide) * cols + lax.rem(index, wide) + start
        hot = spot == high
        inject = None
        for p in range(3):
            left = jnp.where(hot, parts[k, p : p + 1, :], 0.0).astype(jnp.bfloat16)
            term = lax.dot_general(
                left, low_hot[...], (((1,), (1,)), ((), ())), preferred_element_type=jnp.float32
            )
            inject = term if inject is None else inject + term
        inject = inject.reshape(rows, wide, depth)
        window = stress[k, :, pl.ds(start, wide + 2 * PAD), :]
        center = window[:, PAD : PAD + wide]
        zeros = jnp.zeros((4, wide, depth), jnp.float32)
        tall = jnp.concatenate([zeros, center, zeros], axis=0)
        lap = (3.0 * coeffs[0]) * center
        for j in range(1, 5):
            near = window[:, PAD + j : PAD + j + wide] + window[:, PAD - j : PAD - j + wide]
            near = near + (tall[4 + j : 4 + j + rows] + tall[4 - j : 4 - j + rows])
            lap = lap + coeffs[j] * near
            lap = lap + vecs[3 * mechs + j - 1] * pltpu.roll(center, j, 2)
            lap = lap + vecs[3 * mechs + 3 + j] * pltpu.roll(center, depth - j, 2)
        now = adj[:, at, :]
        base[:, at, :] = damp[:, at, :] * (2.0 * now - prev[:, at, :] + lap + inject)
        prev[:, at, :] = now
        total = None
        for m in range(mechs):
            value = vecs[m] * memory[m, :, at, :] + vecs[mechs + m] * now
            memory[m, :, at, :] = value
            total = value if total is None else total + value
        weighted = mod_ref[:, at, :] * total
        relaxed[:, at, :] = relax_ref[:, at, :] * weighted
        gained = grad_t[:, at, :] + weighted * snaps_ref[steps - 1 - k, :, at, :].astype(jnp.float32)
        if last:
            for i in range(per):
                owner = chunk * per + i
                send_t[owner] = gained[:, i * owned : (i + 1) * owned, :]

                @pl.when(owner != me)
                def _(owner=owner):
                    t_copy(owner, me).start()
        else:
            grad_t[:, at, :] = gained

    def after(k, c, last):
        chunk = chunk_of(c)
        start = pl.multiple_of(chunk * wide, wide)
        at = pl.ds(start, wide)
        for side in range(2):
            wait_halo(k, side, start)
            lines = pl.ds(side * half, half)
            near = halo[k, side, :, at, :]
            zeros = jnp.zeros((4, wide, depth), jnp.float32)
            extra = None
            for j in range(1, 5):
                if side == 0:
                    shifted = jnp.concatenate([near, zeros], axis=0)[4 - j : 8 - j]
                else:
                    shifted = jnp.concatenate([zeros, near], axis=0)[j : 4 + j]
                term = coeffs[j] * shifted
                extra = term if extra is None else extra + term
            fresh = base[lines, at, :] + damp[lines, at, :] * extra
            gained = grad_m[lines, at, :] + fresh * snaps_ref[steps - 1 - k, lines, at, :].astype(jnp.float32)
            if last:
                out_ref[0, lines, at, :] = fresh
                for i in range(per):
                    owner = chunk * per + i
                    send_m[owner, lines] = gained[:, i * owned : (i + 1) * owned, :]

                    @pl.when(owner != me)
                    def _(owner=owner, side=side):
                        m_copy(owner, me, side).start()
            else:
                padded = pl.ds(pl.multiple_of(start + PAD, 8), wide)
                stress[k + 1, lines, padded, :] = mod_ref[lines, at, :] * fresh - relaxed[lines, at, :]
                send_halo(k + 1, side, start)
                adj[lines, at, :] = fresh
                grad_m[lines, at, :] = gained

    def loop(k, body, last):
        def one(c, carry):
            body(k, c, last)
            return carry

        lax.fori_loop(0, CHUNKS, one, 0)

    def step(k, carry):
        loop(k, before, False)
        loop(k, after, False)
        return carry

    lax.fori_loop(0, steps - 1, step, 0)
    loop(steps - 1, before, True)
    loop(steps - 1, after, True)

    total_t = send_t[me]
    for away in range(1, shots):
        source = lax.rem(me + away, shots)
        t_copy(source, source).wait_recv()
        total_t = total_t + got_t[source]
    own_t_ref[...] = total_t
    total_m = send_m[me]
    for away in range(1, shots):
        source = lax.rem(me + away, shots)
        for side in range(2):
            m_copy(source, source, side).wait_recv()
        total_m = total_m + got_m[source]
    own_m_ref[...] = total_m

    def finish(k, carry):
        for side in range(2):
            for c in range(CHUNKS):

                @pl.when(has[side])
                def _():
                    halo_copy(k, side, c * wide).wait_send()

        return carry

    lax.fori_loop(0, steps, finish, 0)
    for away in range(1, shots):
        owner = lax.rem(me + away, shots)
        t_copy(owner, me).wait_send()
        for side in range(2):
            m_copy(owner, me, side).wait_send()


def solution(mesh):
    shots = mesh.shape["shot"]
    tiles = mesh.shape["tile"]

    def shards(*args):
        now, _, costates, modulus, _, _, _, _, snaps, cells, _, resid = args
        resid = jnp.transpose(resid, (0, 2, 1, 3))
        rows, cols, depth = modulus.shape
        mechs = costates.shape[1]
        steps = snaps.shape[1]
        receivers = cells.shape[1]
        owned = cols // shots
        field = pltpu.VMEM((rows, cols, depth), jnp.float32)
        blocks = pltpu.VMEM((shots, rows, owned, depth), jnp.float32)
        vmem = pl.BlockSpec(memory_space=pltpu.VMEM)
        hbm = pl.BlockSpec(memory_space=pltpu.HBM)
        smem = pl.BlockSpec(memory_space=pltpu.SMEM)
        return pl.pallas_call(
            functools.partial(kernel, shots, tiles),
            out_shape=(
                jax.ShapeDtypeStruct(now.shape, jnp.float32),
                jax.ShapeDtypeStruct((rows, owned, depth), jnp.float32),
                jax.ShapeDtypeStruct((rows, owned, depth), jnp.float32),
            ),
            in_specs=[hbm] * 6 + [smem] * 2 + [hbm] * 2 + [smem, hbm],
            out_specs=(vmem, vmem, vmem),
            scratch_shapes=[
                pltpu.VMEM((steps, rows, cols + 2 * PAD, depth), jnp.float32),
                pltpu.VMEM((steps, 2, rows // 2, cols, depth), jnp.float32),
                pltpu.VMEM((mechs, rows, cols, depth), jnp.float32),
                field,
                field,
                field,
                field,
                field,
                field,
                field,
                blocks,
                blocks,
                blocks,
                blocks,
                pltpu.VMEM((steps, 8, receivers), jnp.float32),
                pltpu.VMEM((depth, receivers), jnp.bfloat16),
                pltpu.VMEM((3 * mechs + 8, 1, depth), jnp.float32),
                field,
                field,
                pltpu.VMEM((rows, cols, depth), jnp.int32),
                pltpu.VMEM(snaps.shape[1:], snaps.dtype),
                pltpu.VMEM(cells.shape, cells.dtype),
                pltpu.VMEM(resid.shape[1:], resid.dtype),
                pltpu.SemaphoreType.DMA((9,)),
                pltpu.SemaphoreType.DMA((steps, 2, CHUNKS)),
                pltpu.SemaphoreType.DMA((steps, 2, CHUNKS)),
                pltpu.SemaphoreType.DMA((shots, 2)),
                pltpu.SemaphoreType.DMA((shots, 2)),
                pltpu.SemaphoreType.DMA((shots,)),
                pltpu.SemaphoreType.DMA((shots,)),
            ],
            compiler_params=pltpu.CompilerParams(
                collective_id=0, has_side_effects=True, vmem_limit_bytes=63 * 1024 * 1024
            ),
        )(*args[:-1], resid)

    return jax.shard_map(
        shards,
        mesh=mesh,
        in_specs=(
            P("shot", "tile", None, None),
            P("shot", "tile", None, None),
            P("shot", None, "tile", None, None),
            P("tile", None, None),
            P("tile", None, None),
            P("tile", None, None),
            P(),
            P(),
            P("shot", None, "tile", None, None),
            P("shot", None),
            P("shot", None),
            P("shot", None, None, None),
        ),
        out_specs=(P("shot", "tile", None, None), P("tile", "shot", None), P("tile", "shot", None)),
        check_vma=False,
    )
```

```python
import functools

import jax
import jax.numpy as jnp
from jax import lax
from jax.experimental import pallas as pl
from jax.experimental.pallas import tpu as pltpu
from jax.sharding import PartitionSpec as P

MESH = pl.DeviceIdType.MESH
coeffs = (-205.0 / 72.0, 8.0 / 5.0, -1.0 / 5.0, 8.0 / 315.0, -1.0 / 560.0)
damping = 0.2
CHUNKS = 4
PAD = 8


def kernel(
    shots,
    tiles,
    now_hbm,
    prev_hbm,
    cost_hbm,
    mod_hbm,
    relax_hbm,
    mask_hbm,
    rates_ref,
    weights_ref,
    snaps_hbm,
    cells_hbm,
    signs_ref,
    resid_hbm,
    out_ref,
    own_m_ref,
    own_t_ref,
    stress,
    halo,
    memory,
    adj,
    prev,
    damp,
    base,
    relaxed,
    grad_m,
    grad_t,
    send_m,
    send_t,
    got_m,
    got_t,
    parts,
    low_hot,
    vecs,
    mod_ref,
    relax_ref,
    mask_ref,
    snaps_ref,
    cells_ref,
    resid_ref,
    early_loads,
    loads,
    halo_send,
    halo_recv,
    m_send,
    m_recv,
    t_send,
    t_recv,
):
    steps = snaps_ref.shape[0]
    mechs = memory.shape[0]
    rows, cols, depth = mod_ref.shape
    half = rows // 2
    wide = cols // CHUNKS
    per = shots // CHUNKS
    owned = cols // shots
    receivers = cells_ref.shape[1]
    me = lax.axis_index("shot")
    tile = lax.axis_index("tile")
    has = (tile > 0, tile < tiles - 1)
    partner = (tile - 1, tile + 1)

    first = lax.rem(me // per + 1, CHUNKS)

    def chunk_of(c):
        return lax.rem(first + c, CHUNKS)

    def early(c):
        start = pl.multiple_of(chunk_of(c) * wide, wide)
        at = pl.ds(start, wide)
        return [
            pltpu.make_async_copy(source, target, early_loads.at[c, i])
            for i, (source, target) in enumerate(
                (
                    (cost_hbm.at[0, :, :, at, :], memory.at[:, :, at, :]),
                    (now_hbm.at[0, :, at, :], adj.at[:, at, :]),
                    (mod_hbm.at[:, at, :], mod_ref.at[:, at, :]),
                    (relax_hbm.at[:, at, :], relax_ref.at[:, at, :]),
                )
            )
        ]

    for c in range(CHUNKS):
        for load in early(c):
            load.start()

    staged = [
        pltpu.make_async_copy(source, target, loads.at[i])
        for i, (source, target) in enumerate(
            (
                (cells_hbm, cells_ref),
                (resid_hbm.at[0], resid_ref),
                (mask_hbm, mask_ref),
                (prev_hbm.at[0], prev),
                (snaps_hbm.at[0], snaps_ref),
            )
        )
    ]
    for load in staged:
        load.start()

    barrier = pltpu.get_barrier_semaphore()
    for side in range(2):

        @pl.when(has[side])
        def _(side=side):
            pl.semaphore_signal(barrier, inc=1, device_id={"tile": partner[side]}, device_id_type=MESH)

    for away in range(1, shots):
        pl.semaphore_signal(
            barrier, inc=1, device_id={"shot": lax.rem(me + away, shots)}, device_id_type=MESH
        )

    def halo_copy(k, side, start):
        return pltpu.make_async_remote_copy(
            src_ref=stress.at[k, pl.ds(side * half, half), pl.ds(pl.multiple_of(start + PAD, 8), wide), :],
            dst_ref=halo.at[k, 1 - side, :, pl.ds(start, wide), :],
            send_sem=halo_send.at[k, side, start // wide],
            recv_sem=halo_recv.at[k, 1 - side, start // wide],
            device_id={"tile": partner[side]},
            device_id_type=MESH,
        )

    def send_halo(k, side, start):
        @pl.when(has[side])
        def _():
            halo_copy(k, side, start).start()

    def wait_halo(k, side, start):
        @pl.when(has[side])
        def _():
            pltpu.make_async_remote_copy(
                src_ref=stress.at[k, pl.ds(side * half, half), pl.ds(pl.multiple_of(start + PAD, 8), wide), :],
                dst_ref=halo.at[k, side, :, pl.ds(start, wide), :],
                send_sem=halo_send.at[k, side, start // wide],
                recv_sem=halo_recv.at[k, side, start // wide],
                device_id={"tile": partner[side]},
                device_id_type=MESH,
            ).wait_recv()

    def m_copy(owner, source, side):
        return pltpu.make_async_remote_copy(
            src_ref=send_m.at[owner, pl.ds(side * half, half)],
            dst_ref=got_m.at[source, pl.ds(side * half, half)],
            send_sem=m_send.at[owner, side],
            recv_sem=m_recv.at[source, side],
            device_id={"shot": owner},
            device_id_type=MESH,
        )

    def t_copy(owner, source):
        return pltpu.make_async_remote_copy(
            src_ref=send_t.at[owner],
            dst_ref=got_t.at[source],
            send_sem=t_send.at[owner],
            recv_sem=t_recv.at[source],
            device_id={"shot": owner},
            device_id_type=MESH,
        )

    for m in range(mechs):
        decay = jnp.exp(jnp.full((1, depth), -rates_ref[m], jnp.float32))
        weight = jnp.full((1, depth), weights_ref[m], jnp.float32)
        vecs[m] = decay
        vecs[mechs + m] = weight * (1.0 - decay)
        vecs[2 * mechs + m] = weight
    lane = lax.broadcasted_iota(jnp.int32, (1, depth), 1)
    for k in range(1, 5):
        vecs[3 * mechs + k - 1] = jnp.where(lane >= k, coeffs[k], 0.0)
        vecs[3 * mechs + 3 + k] = jnp.where(lane < depth - k, coeffs[k], 0.0)

    def begin_send(c, carry):
        start = pl.multiple_of(chunk_of(c) * wide, wide)
        for side in range(2):
            send_halo(0, side, start)
        return carry

    def begin(c, carry):
        chunk = chunk_of(c)
        start = pl.multiple_of(chunk * wide, wide)
        at = pl.ds(start, wide)
        padded = pl.ds(pl.multiple_of(start + PAD, 8), wide)
        for load in early(c):
            load.wait()
        total = None
        for m in range(mechs):
            value = vecs[2 * mechs + m] * memory[m, :, at, :]
            memory[m, :, at, :] = value
            total = value if total is None else total + value
        now = adj[:, at, :]
        stress[0, :, padded, :] = mod_ref[:, at, :] * (now - relax_ref[:, at, :] * total)
        return carry

    begin(0, 0)
    peers = shots - 1 + has[0].astype(jnp.int32) + has[1].astype(jnp.int32)
    pl.semaphore_wait(barrier, peers)
    begin_send(0, 0)

    def begin_both(c, carry):
        begin(c, carry)
        return begin_send(c, carry)

    lax.fori_loop(1, CHUNKS, begin_both, 0)

    empty = jnp.zeros((rows, PAD, depth), jnp.float32)

    def clear(k, carry):
        stress[k, :, 0:PAD, :] = empty
        stress[k, :, PAD + cols :, :] = empty
        for side in range(2):

            @pl.when(jnp.logical_not(has[side]))
            def _(side=side):
                halo[k, side] = jnp.zeros((half, cols, depth), jnp.float32)

        return carry

    lax.fori_loop(0, steps, clear, 0)

    for load in staged[:2]:
        load.wait()
    sources = None
    for e in range(signs_ref.shape[1]):
        term = signs_ref[0, e].astype(jnp.float32) * resid_ref[:, e]
        sources = term if sources is None else sources + term
    for p in range(3):
        piece = sources.astype(jnp.bfloat16).astype(jnp.float32)
        for k in range(steps):
            parts[k, p : p + 1, :] = piece[steps - 1 - k : steps - k]
        sources = sources - piece
    cell = cells_ref[...] - tile * (rows * cols * depth)
    high = cell >> 7
    low = cell & 127
    low_hot[...] = jnp.where(
        lax.broadcasted_iota(jnp.int32, (depth, receivers), 0) == low, 1.0, 0.0
    ).astype(jnp.bfloat16)

    for load in staged[2:]:
        load.wait()

    def prepare(c, carry):
        at = pl.ds(pl.multiple_of(c * wide, wide), wide)
        damp[:, at, :] = 1.0 - damping * mask_ref[:, at, :].astype(jnp.float32)
        grad_m[:, at, :] = jnp.zeros((rows, wide, depth), jnp.float32)
        grad_t[:, at, :] = jnp.zeros((rows, wide, depth), jnp.float32)
        return carry

    lax.fori_loop(0, CHUNKS, prepare, 0)

    def local(k, c, last):
        chunk = chunk_of(c)
        start = pl.multiple_of(chunk * wide, wide)
        at = pl.ds(start, wide)
        index = lax.broadcasted_iota(jnp.int32, (rows * wide, receivers), 0)
        spot = (index // wide) * cols + lax.rem(index, wide) + start
        hot = spot == high
        inject = None
        for p in range(3):
            left = jnp.where(hot, parts[k, p : p + 1, :], 0.0).astype(jnp.bfloat16)
            term = lax.dot_general(
                left, low_hot[...], (((1,), (1,)), ((), ())), preferred_element_type=jnp.float32
            )
            inject = term if inject is None else inject + term
        inject = inject.reshape(rows, wide, depth)
        now = adj[:, at, :]
        base[:, at, :] = 2.0 * now - prev[:, at, :] + inject
        prev[:, at, :] = now
        total = None
        for m in range(mechs):
            value = vecs[m] * memory[m, :, at, :] + vecs[mechs + m] * now
            memory[m, :, at, :] = value
            total = value if total is None else total + value
        weighted = mod_ref[:, at, :] * total
        relaxed[:, at, :] = relax_ref[:, at, :] * weighted
        gained = grad_t[:, at, :] + weighted * snaps_ref[steps - 1 - k, :, at, :].astype(jnp.float32)
        if last:
            for i in range(per):
                owner = chunk * per + i
                send_t[owner] = gained[:, i * owned : (i + 1) * owned, :]

                @pl.when(owner != me)
                def _(owner=owner):
                    t_copy(owner, me).start()
        else:
            grad_t[:, at, :] = gained

    def across(k, c):
        start = pl.multiple_of(chunk_of(c) * wide, wide)
        at = pl.ds(start, wide)
        window = stress[k, :, pl.ds(start, wide + 2 * PAD), :]
        center = window[:, PAD : PAD + wide]
        zeros = jnp.zeros((4, wide, depth), jnp.float32)
        tall = jnp.concatenate([zeros, center, zeros], axis=0)
        lap = (3.0 * coeffs[0]) * center
        for j in range(1, 5):
            near = window[:, PAD + j : PAD + j + wide] + window[:, PAD - j : PAD - j + wide]
            near = near + (tall[4 + j : 4 + j + rows] + tall[4 - j : 4 - j + rows])
            lap = lap + coeffs[j] * near
            lap = lap + vecs[3 * mechs + j - 1] * pltpu.roll(center, j, 2)
            lap = lap + vecs[3 * mechs + 3 + j] * pltpu.roll(center, depth - j, 2)
        base[:, at, :] = damp[:, at, :] * (base[:, at, :] + lap)

    def after(k, c, last):
        chunk = chunk_of(c)
        start = pl.multiple_of(chunk * wide, wide)
        at = pl.ds(start, wide)
        for side in range(2):
            wait_halo(k, side, start)
            lines = pl.ds(side * half, half)
            near = halo[k, side, :, at, :]
            zeros = jnp.zeros((4, wide, depth), jnp.float32)
            extra = None
            for j in range(1, 5):
                if side == 0:
                    shifted = jnp.concatenate([near, zeros], axis=0)[4 - j : 8 - j]
                else:
                    shifted = jnp.concatenate([zeros, near], axis=0)[j : 4 + j]
                term = coeffs[j] * shifted
                extra = term if extra is None else extra + term
            fresh = base[lines, at, :] + damp[lines, at, :] * extra
            gained = grad_m[lines, at, :] + fresh * snaps_ref[steps - 1 - k, lines, at, :].astype(jnp.float32)
            if last:
                out_ref[0, lines, at, :] = fresh
                for i in range(per):
                    owner = chunk * per + i
                    send_m[owner, lines] = gained[:, i * owned : (i + 1) * owned, :]

                    @pl.when(owner != me)
                    def _(owner=owner, side=side):
                        m_copy(owner, me, side).start()
            else:
                padded = pl.ds(pl.multiple_of(start + PAD, 8), wide)
                stress[k + 1, lines, padded, :] = mod_ref[lines, at, :] * fresh - relaxed[lines, at, :]
                send_halo(k + 1, side, start)
                adj[lines, at, :] = fresh
                grad_m[lines, at, :] = gained

    def each(body):
        def one(c, carry):
            body(c)
            return carry

        lax.fori_loop(0, CHUNKS, one, 0)

    def step(k, last):
        def one(c):
            after(k, c, False)
            local(k + 1, c, last)

        each(one)
        each(lambda c: across(k + 1, c))

    each(lambda c: local(0, c, False))
    each(lambda c: across(0, c))

    def middle(k, carry):
        step(k, False)
        return carry

    lax.fori_loop(0, steps - 2, middle, 0)
    step(steps - 2, True)

    def finish(k, carry):
        for side in range(2):
            for c in range(CHUNKS):

                @pl.when(has[side])
                def _():
                    halo_copy(k, side, c * wide).wait_send()

        return carry

    lax.fori_loop(0, steps - 1, finish, 0)
    each(lambda c: after(steps - 1, c, True))

    total_t = send_t[me]
    for away in range(1, shots):
        source = lax.rem(me + away, shots)
        t_copy(source, source).wait_recv()
        total_t = total_t + got_t[source]
    own_t_ref[...] = total_t
    total_m = send_m[me]
    for away in range(1, shots):
        source = lax.rem(me + away, shots)
        for side in range(2):
            m_copy(source, source, side).wait_recv()
        total_m = total_m + got_m[source]
    own_m_ref[...] = total_m

    finish(steps - 1, 0)
    for away in range(1, shots):
        owner = lax.rem(me + away, shots)
        t_copy(owner, me).wait_send()
        for side in range(2):
            m_copy(owner, me, side).wait_send()


def store(a, b, c, to_a, to_b, to_c, sems):
    copies = [
        pltpu.make_async_copy(source, target, sems.at[i])
        for i, (source, target) in enumerate(((a, to_a), (b, to_b), (c, to_c)))
    ]
    for copy in copies:
        copy.start()
    for copy in copies:
        copy.wait()


def solution(mesh):
    shots = mesh.shape["shot"]
    tiles = mesh.shape["tile"]

    def shards(*args):
        now, _, costates, modulus, _, _, _, _, snaps, cells, _, resid = args
        resid = jnp.transpose(resid, (0, 2, 1, 3))
        rows, cols, depth = modulus.shape
        mechs = costates.shape[1]
        steps = snaps.shape[1]
        receivers = cells.shape[1]
        owned = cols // shots
        field = pltpu.VMEM((rows, cols, depth), jnp.float32)
        blocks = pltpu.VMEM((shots, rows, owned, depth), jnp.float32)
        vmem = pl.BlockSpec(memory_space=pltpu.VMEM)
        hbm = pl.BlockSpec(memory_space=pltpu.HBM)
        smem = pl.BlockSpec(memory_space=pltpu.SMEM)
        results = pl.pallas_call(
            functools.partial(kernel, shots, tiles),
            out_shape=(
                pltpu.VMEM(now.shape, jnp.float32),
                pltpu.VMEM((rows, owned, depth), jnp.float32),
                pltpu.VMEM((rows, owned, depth), jnp.float32),
            ),
            in_specs=[hbm] * 6 + [smem] * 2 + [hbm] * 2 + [smem, hbm],
            out_specs=(vmem, vmem, vmem),
            scratch_shapes=[
                pltpu.VMEM((steps, rows, cols + 2 * PAD, depth), jnp.float32),
                pltpu.VMEM((steps, 2, rows // 2, cols, depth), jnp.float32),
                pltpu.VMEM((mechs, rows, cols, depth), jnp.float32),
                field,
                field,
                field,
                field,
                field,
                field,
                field,
                blocks,
                blocks,
                blocks,
                blocks,
                pltpu.VMEM((steps, 8, receivers), jnp.float32),
                pltpu.VMEM((depth, receivers), jnp.bfloat16),
                pltpu.VMEM((3 * mechs + 8, 1, depth), jnp.float32),
                field,
                field,
                pltpu.VMEM((rows, cols, depth), jnp.int32),
                pltpu.VMEM(snaps.shape[1:], snaps.dtype),
                pltpu.VMEM(cells.shape, cells.dtype),
                pltpu.VMEM(resid.shape[1:], resid.dtype),
                pltpu.SemaphoreType.DMA((CHUNKS, 4)),
                pltpu.SemaphoreType.DMA((5,)),
                pltpu.SemaphoreType.DMA((steps, 2, CHUNKS)),
                pltpu.SemaphoreType.DMA((steps, 2, CHUNKS)),
                pltpu.SemaphoreType.DMA((shots, 2)),
                pltpu.SemaphoreType.DMA((shots, 2)),
                pltpu.SemaphoreType.DMA((shots,)),
                pltpu.SemaphoreType.DMA((shots,)),
            ],
            compiler_params=pltpu.CompilerParams(
                collective_id=0, has_side_effects=True, vmem_limit_bytes=63 * 1024 * 1024
            ),
        )(*args[:-1], resid)
        return pl.pallas_call(
            store,
            out_shape=[jax.ShapeDtypeStruct(r.shape, r.dtype) for r in results],
            in_specs=[vmem] * 3,
            out_specs=[pl.BlockSpec(memory_space=pl.ANY)] * 3,
            scratch_shapes=[pltpu.SemaphoreType.DMA((3,))],
        )(*[pltpu.with_memory_space_constraint(r, pltpu.VMEM) for r in results])

    return jax.shard_map(
        shards,
        mesh=mesh,
        in_specs=(
            P("shot", "tile", None, None),
            P("shot", "tile", None, None),
            P("shot", None, "tile", None, None),
            P("tile", None, None),
            P("tile", None, None),
            P("tile", None, None),
            P(),
            P(),
            P("shot", None, "tile", None, None),
            P("shot", None),
            P("shot", None),
            P("shot", None, None, None),
        ),
        out_specs=(P("shot", "tile", None, None), P("tile", "shot", None), P("tile", "shot", None)),
        check_vma=False,
    )
```

```python
import functools

import jax
import jax.numpy as jnp
from jax import lax
from jax.experimental import pallas as pl
from jax.experimental.pallas import tpu as pltpu
from jax.sharding import PartitionSpec as P

MESH = pl.DeviceIdType.MESH
coeffs = (-205.0 / 72.0, 8.0 / 5.0, -1.0 / 5.0, 8.0 / 315.0, -1.0 / 560.0)
damping = 0.2
CHUNKS = 4
PAD = 8


def kernel(
    shots,
    tiles,
    now_hbm,
    prev_hbm,
    cost_hbm,
    mod_hbm,
    relax_hbm,
    mask_hbm,
    rates_ref,
    weights_ref,
    snaps_hbm,
    cells_hbm,
    signs_ref,
    resid_hbm,
    out_ref,
    own_m_ref,
    own_t_ref,
    stress,
    halo,
    memory,
    adj,
    prev,
    damp,
    base,
    relaxed,
    grad_m,
    grad_t,
    send_m,
    send_t,
    got_m,
    got_t,
    parts,
    low_hot,
    vecs,
    mod_ref,
    relax_ref,
    mask_ref,
    snaps_ref,
    cells_ref,
    resid_ref,
    early_loads,
    loads,
    halo_send,
    halo_recv,
    m_send,
    m_recv,
    t_send,
    t_recv,
):
    steps = snaps_ref.shape[0]
    mechs = memory.shape[0]
    rows, cols, depth = mod_ref.shape
    half = rows // 2
    wide = cols // CHUNKS
    per = shots // CHUNKS
    owned = cols // shots
    receivers = cells_ref.shape[1]
    me = lax.axis_index("shot")
    tile = lax.axis_index("tile")
    has = (tile > 0, tile < tiles - 1)
    partner = (tile - 1, tile + 1)

    first = lax.rem(me // per + 1, CHUNKS)

    def chunk_of(c):
        return lax.rem(first + c, CHUNKS)

    def early(c):
        start = pl.multiple_of(chunk_of(c) * wide, wide)
        at = pl.ds(start, wide)
        return [
            pltpu.make_async_copy(source, target, early_loads.at[c, i])
            for i, (source, target) in enumerate(
                (
                    (cost_hbm.at[0, :, :, at, :], memory.at[:, :, at, :]),
                    (now_hbm.at[0, :, at, :], adj.at[:, at, :]),
                    (mod_hbm.at[:, at, :], mod_ref.at[:, at, :]),
                    (relax_hbm.at[:, at, :], relax_ref.at[:, at, :]),
                )
            )
        ]

    for c in range(CHUNKS):
        for load in early(c):
            load.start()

    staged = [
        pltpu.make_async_copy(source, target, loads.at[i])
        for i, (source, target) in enumerate(
            (
                (cells_hbm, cells_ref),
                (resid_hbm.at[0], resid_ref),
                (mask_hbm, mask_ref),
                (prev_hbm.at[0], prev),
                (snaps_hbm.at[0], snaps_ref),
            )
        )
    ]
    for load in staged:
        load.start()

    barrier = pltpu.get_barrier_semaphore()
    for side in range(2):

        @pl.when(has[side])
        def _(side=side):
            pl.semaphore_signal(barrier, inc=1, device_id={"tile": partner[side]}, device_id_type=MESH)

    for away in range(1, shots):
        pl.semaphore_signal(
            barrier, inc=1, device_id={"shot": lax.rem(me + away, shots)}, device_id_type=MESH
        )

    def halo_copy(k, side, start):
        return pltpu.make_async_remote_copy(
            src_ref=stress.at[k, pl.ds(side * half, half), pl.ds(pl.multiple_of(start + PAD, 8), wide), :],
            dst_ref=halo.at[k, 1 - side, :, pl.ds(start, wide), :],
            send_sem=halo_send.at[k, side, start // wide],
            recv_sem=halo_recv.at[k, 1 - side, start // wide],
            device_id={"tile": partner[side]},
            device_id_type=MESH,
        )

    def send_halo(k, side, start):
        @pl.when(has[side])
        def _():
            halo_copy(k, side, start).start()

    def wait_halo(k, side, start):
        @pl.when(has[side])
        def _():
            pltpu.make_async_remote_copy(
                src_ref=stress.at[k, pl.ds(side * half, half), pl.ds(pl.multiple_of(start + PAD, 8), wide), :],
                dst_ref=halo.at[k, side, :, pl.ds(start, wide), :],
                send_sem=halo_send.at[k, side, start // wide],
                recv_sem=halo_recv.at[k, side, start // wide],
                device_id={"tile": partner[side]},
                device_id_type=MESH,
            ).wait_recv()

    def m_copy(owner, source, side):
        return pltpu.make_async_remote_copy(
            src_ref=send_m.at[owner, pl.ds(side * half, half)],
            dst_ref=got_m.at[source, pl.ds(side * half, half)],
            send_sem=m_send.at[owner, side],
            recv_sem=m_recv.at[source, side],
            device_id={"shot": owner},
            device_id_type=MESH,
        )

    def t_copy(owner, source):
        return pltpu.make_async_remote_copy(
            src_ref=send_t.at[owner],
            dst_ref=got_t.at[source],
            send_sem=t_send.at[owner],
            recv_sem=t_recv.at[source],
            device_id={"shot": owner},
            device_id_type=MESH,
        )

    for m in range(mechs):
        decay = jnp.exp(jnp.full((1, depth), -rates_ref[m], jnp.float32))
        weight = jnp.full((1, depth), weights_ref[m], jnp.float32)
        vecs[m] = decay
        vecs[mechs + m] = weight * (1.0 - decay)
        vecs[2 * mechs + m] = weight
    lane = lax.broadcasted_iota(jnp.int32, (1, depth), 1)
    for k in range(1, 5):
        vecs[3 * mechs + k - 1] = jnp.where(lane >= k, coeffs[k], 0.0)
        vecs[3 * mechs + 3 + k] = jnp.where(lane < depth - k, coeffs[k], 0.0)

    def begin_send(c, carry):
        start = pl.multiple_of(chunk_of(c) * wide, wide)
        for side in range(2):
            send_halo(0, side, start)
        return carry

    def begin(c, carry):
        chunk = chunk_of(c)
        start = pl.multiple_of(chunk * wide, wide)
        at = pl.ds(start, wide)
        padded = pl.ds(pl.multiple_of(start + PAD, 8), wide)
        for load in early(c):
            load.wait()
        total = None
        for m in range(mechs):
            value = vecs[2 * mechs + m] * memory[m, :, at, :]
            memory[m, :, at, :] = value
            total = value if total is None else total + value
        now = adj[:, at, :]
        stress[0, :, padded, :] = mod_ref[:, at, :] * (now - relax_ref[:, at, :] * total)
        return carry

    begin(0, 0)
    peers = shots - 1 + has[0].astype(jnp.int32) + has[1].astype(jnp.int32)
    pl.semaphore_wait(barrier, peers)
    begin_send(0, 0)

    def begin_both(c, carry):
        begin(c, carry)
        return begin_send(c, carry)

    lax.fori_loop(1, CHUNKS, begin_both, 0)

    empty = jnp.zeros((rows, PAD, depth), jnp.float32)

    def clear(k, carry):
        stress[k, :, 0:PAD, :] = empty
        stress[k, :, PAD + cols :, :] = empty
        for side in range(2):

            @pl.when(jnp.logical_not(has[side]))
            def _(side=side):
                halo[k, side] = jnp.zeros((half, cols, depth), jnp.float32)

        return carry

    lax.fori_loop(0, steps, clear, 0)

    for load in staged[:2]:
        load.wait()
    sources = None
    for e in range(signs_ref.shape[1]):
        term = signs_ref[0, e].astype(jnp.float32) * resid_ref[:, e]
        sources = term if sources is None else sources + term
    for p in range(3):
        piece = sources.astype(jnp.bfloat16).astype(jnp.float32)
        for k in range(steps):
            parts[k, p : p + 1, :] = piece[steps - 1 - k : steps - k]
        sources = sources - piece
    cell = cells_ref[...] - tile * (rows * cols * depth)
    high = cell >> 7
    low = cell & 127
    low_hot[...] = jnp.where(
        lax.broadcasted_iota(jnp.int32, (depth, receivers), 0) == low, 1.0, 0.0
    ).astype(jnp.bfloat16)

    for load in staged[2:]:
        load.wait()

    def prepare(c, carry):
        at = pl.ds(pl.multiple_of(c * wide, wide), wide)
        damp[:, at, :] = 1.0 - damping * mask_ref[:, at, :].astype(jnp.float32)
        grad_m[:, at, :] = jnp.zeros((rows, wide, depth), jnp.float32)
        grad_t[:, at, :] = jnp.zeros((rows, wide, depth), jnp.float32)
        return carry

    lax.fori_loop(0, CHUNKS, prepare, 0)

    def local(k, c, last):
        chunk = chunk_of(c)
        start = pl.multiple_of(chunk * wide, wide)
        at = pl.ds(start, wide)
        index = lax.broadcasted_iota(jnp.int32, (rows * wide, receivers), 0)
        spot = (index // wide) * cols + lax.rem(index, wide) + start
        hot = spot == high
        inject = None
        for p in range(3):
            left = jnp.where(hot, parts[k, p : p + 1, :], 0.0).astype(jnp.bfloat16)
            term = lax.dot_general(
                left, low_hot[...], (((1,), (1,)), ((), ())), preferred_element_type=jnp.float32
            )
            inject = term if inject is None else inject + term
        inject = inject.reshape(rows, wide, depth)
        now = adj[:, at, :]
        base[:, at, :] = 2.0 * now - prev[:, at, :] + inject
        prev[:, at, :] = now
        total = None
        for m in range(mechs):
            value = vecs[m] * memory[m, :, at, :] + vecs[mechs + m] * now
            memory[m, :, at, :] = value
            total = value if total is None else total + value
        weighted = mod_ref[:, at, :] * total
        relaxed[:, at, :] = relax_ref[:, at, :] * weighted
        gained = grad_t[:, at, :] + weighted * snaps_ref[steps - 1 - k, :, at, :].astype(jnp.float32)
        if last:
            for i in range(per):
                owner = chunk * per + i
                send_t[owner] = gained[:, i * owned : (i + 1) * owned, :]

                @pl.when(owner != me)
                def _(owner=owner):
                    t_copy(owner, me).start()
        else:
            grad_t[:, at, :] = gained

    def across(k, c):
        start = pl.multiple_of(chunk_of(c) * wide, wide)
        at = pl.ds(start, wide)
        window = stress[k, :, pl.ds(start, wide + 2 * PAD), :]
        center = window[:, PAD : PAD + wide]
        zeros = jnp.zeros((4, wide, depth), jnp.float32)
        tall = jnp.concatenate([zeros, center, zeros], axis=0)
        lap = (3.0 * coeffs[0]) * center
        for j in range(1, 5):
            near = window[:, PAD + j : PAD + j + wide] + window[:, PAD - j : PAD - j + wide]
            near = near + (tall[4 + j : 4 + j + rows] + tall[4 - j : 4 - j + rows])
            lap = lap + coeffs[j] * near
            lap = lap + vecs[3 * mechs + j - 1] * pltpu.roll(center, j, 2)
            lap = lap + vecs[3 * mechs + 3 + j] * pltpu.roll(center, depth - j, 2)
        base[:, at, :] = damp[:, at, :] * (base[:, at, :] + lap)

    def after(k, c, last):
        chunk = chunk_of(c)
        start = pl.multiple_of(chunk * wide, wide)
        at = pl.ds(start, wide)
        for side in range(2):
            wait_halo(k, side, start)
            lines = pl.ds(side * half, half)
            near = halo[k, side, :, at, :]
            zeros = jnp.zeros((4, wide, depth), jnp.float32)
            extra = None
            for j in range(1, 5):
                if side == 0:
                    shifted = jnp.concatenate([near, zeros], axis=0)[4 - j : 8 - j]
                else:
                    shifted = jnp.concatenate([zeros, near], axis=0)[j : 4 + j]
                term = coeffs[j] * shifted
                extra = term if extra is None else extra + term
            fresh = base[lines, at, :] + damp[lines, at, :] * extra
            gained = grad_m[lines, at, :] + fresh * snaps_ref[steps - 1 - k, lines, at, :].astype(jnp.float32)
            if last:
                out_ref[0, lines, at, :] = fresh
                for i in range(per):
                    owner = chunk * per + i
                    send_m[owner, lines] = gained[:, i * owned : (i + 1) * owned, :]

                    @pl.when(owner != me)
                    def _(owner=owner, side=side):
                        m_copy(owner, me, side).start()
            else:
                padded = pl.ds(pl.multiple_of(start + PAD, 8), wide)
                stress[k + 1, lines, padded, :] = mod_ref[lines, at, :] * fresh - relaxed[lines, at, :]
                send_halo(k + 1, side, start)
                adj[lines, at, :] = fresh
                grad_m[lines, at, :] = gained

    def each(body):
        def one(c, carry):
            body(c)
            return carry

        lax.fori_loop(0, CHUNKS, one, 0)

    def step(k, last):
        def one(c):
            after(k, c, False)
            local(k + 1, c, last)

        each(one)
        each(lambda c: across(k + 1, c))

    each(lambda c: local(0, c, False))
    each(lambda c: across(0, c))

    def middle(k, carry):
        step(k, False)
        return carry

    lax.fori_loop(0, steps - 2, middle, 0)
    step(steps - 2, True)

    def finish(k, carry):
        for side in range(2):
            for c in range(CHUNKS):

                @pl.when(has[side])
                def _():
                    halo_copy(k, side, c * wide).wait_send()

        return carry

    lax.fori_loop(0, steps - 1, finish, 0)
    def closing(c, carry):
        after(steps - 1, c, True)
        return carry

    lax.fori_loop(0, CHUNKS - 1, closing, 0)
    total_t = send_t[me]
    for away in range(1, shots):
        source = lax.rem(me + away, shots)
        t_copy(source, source).wait_recv()
        total_t = total_t + got_t[source]
    own_t_ref[...] = total_t
    after(steps - 1, CHUNKS - 1, True)

    total_m = send_m[me]
    for away in range(1, shots):
        source = lax.rem(me + away, shots)
        for side in range(2):
            m_copy(source, source, side).wait_recv()
        total_m = total_m + got_m[source]
    own_m_ref[...] = total_m

    finish(steps - 1, 0)
    for away in range(1, shots):
        owner = lax.rem(me + away, shots)
        t_copy(owner, me).wait_send()
        for side in range(2):
            m_copy(owner, me, side).wait_send()


def store(a, b, c, to_a, to_b, to_c, sems):
    copies = [
        pltpu.make_async_copy(source, target, sems.at[i])
        for i, (source, target) in enumerate(((a, to_a), (b, to_b), (c, to_c)))
    ]
    for copy in copies:
        copy.start()
    for copy in copies:
        copy.wait()


def solution(mesh):
    shots = mesh.shape["shot"]
    tiles = mesh.shape["tile"]

    def shards(*args):
        now, _, costates, modulus, _, _, _, _, snaps, cells, _, resid = args
        resid = jnp.transpose(resid, (0, 2, 1, 3))
        rows, cols, depth = modulus.shape
        mechs = costates.shape[1]
        steps = snaps.shape[1]
        receivers = cells.shape[1]
        owned = cols // shots
        field = pltpu.VMEM((rows, cols, depth), jnp.float32)
        blocks = pltpu.VMEM((shots, rows, owned, depth), jnp.float32)
        vmem = pl.BlockSpec(memory_space=pltpu.VMEM)
        hbm = pl.BlockSpec(memory_space=pltpu.HBM)
        smem = pl.BlockSpec(memory_space=pltpu.SMEM)
        results = pl.pallas_call(
            functools.partial(kernel, shots, tiles),
            out_shape=(
                pltpu.VMEM(now.shape, jnp.float32),
                pltpu.VMEM((rows, owned, depth), jnp.float32),
                pltpu.VMEM((rows, owned, depth), jnp.float32),
            ),
            in_specs=[hbm] * 6 + [smem] * 2 + [hbm] * 2 + [smem, hbm],
            out_specs=(vmem, vmem, vmem),
            scratch_shapes=[
                pltpu.VMEM((steps, rows, cols + 2 * PAD, depth), jnp.float32),
                pltpu.VMEM((steps, 2, rows // 2, cols, depth), jnp.float32),
                pltpu.VMEM((mechs, rows, cols, depth), jnp.float32),
                field,
                field,
                field,
                field,
                field,
                field,
                field,
                blocks,
                blocks,
                blocks,
                blocks,
                pltpu.VMEM((steps, 8, receivers), jnp.float32),
                pltpu.VMEM((depth, receivers), jnp.bfloat16),
                pltpu.VMEM((3 * mechs + 8, 1, depth), jnp.float32),
                field,
                field,
                pltpu.VMEM((rows, cols, depth), jnp.int32),
                pltpu.VMEM(snaps.shape[1:], snaps.dtype),
                pltpu.VMEM(cells.shape, cells.dtype),
                pltpu.VMEM(resid.shape[1:], resid.dtype),
                pltpu.SemaphoreType.DMA((CHUNKS, 4)),
                pltpu.SemaphoreType.DMA((5,)),
                pltpu.SemaphoreType.DMA((steps, 2, CHUNKS)),
                pltpu.SemaphoreType.DMA((steps, 2, CHUNKS)),
                pltpu.SemaphoreType.DMA((shots, 2)),
                pltpu.SemaphoreType.DMA((shots, 2)),
                pltpu.SemaphoreType.DMA((shots,)),
                pltpu.SemaphoreType.DMA((shots,)),
            ],
            compiler_params=pltpu.CompilerParams(
                collective_id=0, has_side_effects=True, vmem_limit_bytes=63 * 1024 * 1024
            ),
        )(*args[:-1], resid)
        return pl.pallas_call(
            store,
            out_shape=[jax.ShapeDtypeStruct(r.shape, r.dtype) for r in results],
            in_specs=[vmem] * 3,
            out_specs=[pl.BlockSpec(memory_space=pl.ANY)] * 3,
            scratch_shapes=[pltpu.SemaphoreType.DMA((3,))],
        )(*[pltpu.with_memory_space_constraint(r, pltpu.VMEM) for r in results])

    return jax.shard_map(
        shards,
        mesh=mesh,
        in_specs=(
            P("shot", "tile", None, None),
            P("shot", "tile", None, None),
            P("shot", None, "tile", None, None),
            P("tile", None, None),
            P("tile", None, None),
            P("tile", None, None),
            P(),
            P(),
            P("shot", None, "tile", None, None),
            P("shot", None),
            P("shot", None),
            P("shot", None, None, None),
        ),
        out_specs=(P("shot", "tile", None, None), P("tile", "shot", None), P("tile", "shot", None)),
        check_vma=False,
    )
```
